128 devices in a mesh: feed: 32 (over y_hi, x, z), tm: 4 (over y_lo, core).
Axes of the slice: x: 4, y: 4 (y_hi: 2, y_lo: 2; y = y_hi * 2 + y_lo), z: 4, core: 2. Of those that a mesh axis runs over, the one named last changes fastest.
Arguments:
- voltages: int32 [512, 524288], P('feed', 'tm'), may hold values from -128 to 127, as said below
- pfb_taps: float32 [16, 2048], replicated, may hold values from -3 to 3
- feed_flags: int32 [512], P('feed'), may hold values 0 or 1
Outputs:
- visibility: float32 [1024, 2, 512, 512], P(('feed', 'tm'))
The draws below stay inside these ranges and needn't reach their ends.
Inputs may be any that keep to these rules, and one draw needn't show every extreme that they name: `voltages`: signed 8-bit sample values.
All inputs are finite; a program needn't handle non-finite values. No bound on the sum of `feed_flags` on one device may be relied on, other than what follows from the above.
Results may differ from the reference program's by a relative error of at most 0.0019.
Values may be sent and summed in bfloat16 or wider, within the bound.
A program may use at most 128 MiB of HBM per device.

```python
import math
import jax
import jax.numpy as jnp
from jax import lax

INPUTS = 512
CH = 1024
TAPS = 16
FRAME = 2048
SPECTRA = 256
SAMPLES = 524288


def draw_voltages(key, part):
    common_key = jax.random.fold_in(key, 11)
    gain_key = jax.random.fold_in(key, 23)
    noise_key = jax.random.fold_in(key, 37)
    common = jax.random.randint(common_key, (1, SAMPLES), -48, 49)
    gain_steps = jax.random.randint(gain_key, (INPUTS, 1), -3, 4)
    noise_part = jax.random.randint(noise_key, (INPUTS, SAMPLES), -64, 65)
    return jnp.clip(gain_steps * common + noise_part, -128, 127).astype(jnp.int32)


def touch_ends(array, rng, low, largest):
    index_at = [jax.random.randint(jax.random.fold_in(rng, axis), (), 0, length) for axis, length in enumerate(array.shape)]
    main_axis = array.shape.index(max(array.shape))
    next_to = index_at[:main_axis] + [(index_at[main_axis] + 1) % array.shape[main_axis]] + index_at[main_axis + 1:]
    return array.at[tuple(index_at)].set(low).at[tuple(next_to)].set(largest)


def gaussian(own_key, extent, width, most, dtype=jnp.bfloat16):
    return jnp.clip(width * jax.random.normal(own_key, extent, jnp.float32), -most, most).astype(dtype)


def setup_inputs(seed: int = 0) -> dict:
    splits = jax.random.split(jax.random.key(seed), 4)
    voltages = draw_voltages(jax.random.fold_in(splits[3], 71), 0)
    pfb_taps = gaussian(splits[1], (TAPS, FRAME), 0.5, 3.0, jnp.float32)
    feed_flags = touch_ends((jax.random.randint(splits[2], (INPUTS,), 0, 8) < 7).astype(jnp.int32), jax.random.fold_in(splits[2], 1), 0, 1)
    return {"voltages": voltages, "pfb_taps": pfb_taps, "feed_flags": feed_flags}


def correlate(block):
    values = block.astype(jnp.float32)
    swapped = jnp.stack([values[:, 1], -values[:, 0]], axis=1)
    vis_real = jnp.einsum('cris,crjs->cij', values, values, precision=lax.Precision.HIGHEST)
    vis_imag = jnp.einsum('cris,crjs->cij', swapped, values, precision=lax.Precision.HIGHEST)
    return jnp.stack([vis_real, vis_imag], axis=1) / SPECTRA

def reference(voltages, pfb_taps, feed_flags):
    frames = (voltages.astype(jnp.float32) / 128.0).reshape(INPUTS, SPECTRA, FRAME)
    padded = jnp.concatenate([jnp.zeros((INPUTS, TAPS - 1, FRAME), jnp.float32), frames], axis=1)
    running = jnp.zeros((INPUTS, SPECTRA, FRAME), jnp.float32)
    for tap_lag in range(TAPS):
        offset = TAPS - 1 - tap_lag
        running = running + pfb_taps[tap_lag] * padded[:, offset:offset + SPECTRA, :]
    kept_mask = feed_flags.astype(jnp.float32)[:, None, None]
    filtered = (running * kept_mask).astype(jnp.bfloat16)
    spectrum = jnp.fft.rfft(filtered.astype(jnp.float32), axis=-1)[:, :, :CH] / math.sqrt(FRAME)
    real_part = jnp.real(spectrum).astype(jnp.bfloat16)
    imag_part = jnp.imag(spectrum).astype(jnp.bfloat16)
    stacked = jnp.stack([real_part, imag_part])
    block_len = min(64, CH)
    stacked = jnp.transpose(stacked, (3, 0, 1, 2)).reshape(CH // block_len, block_len, 2, INPUTS, SPECTRA)
    result = lax.map(correlate, stacked)
    return result.reshape(CH, 2, INPUTS, INPUTS)
```

```python
import functools
import math

import jax
import jax.numpy as jnp
import numpy as np
from jax import lax
from jax.experimental import pallas as pl
from jax.experimental.pallas import tpu as pltpu
from jax.sharding import PartitionSpec as P

LANES = 128
RADIX = 16


def coefficient_tables(frame_len):
    fine = frame_len // RADIX
    keep = fine // 2
    n2 = np.arange(fine)[None, :]
    k2 = np.arange(keep)[:, None]

    def wave(k1):
        phase = (k1 + RADIX * k2) * n2 % frame_len
        angle = phase * (2.0 * np.pi / frame_len)
        return np.cos(angle), np.sin(angle)

    zero = np.zeros((keep, fine))
    groups = []
    c0, s0 = wave(0)
    c8, s8 = wave(RADIX // 2)
    groups.append(np.block([[c0, zero], [-s0, zero], [zero, c8], [zero, -s8]]))
    for g in range(1, RADIX // 2):
        c, s = wave(g)
        d, t = wave(RADIX - g)
        groups.append(np.block([[c, s], [-s, c], [d, -t], [-t, -d]]))
    table = (np.stack(groups) / math.sqrt(frame_len)).astype(np.float32)
    high = table.astype(jnp.bfloat16)
    low = (table - high.astype(np.float32)).astype(jnp.bfloat16)
    return high, low


def real_dft16(x):
    R = np.float32(math.sqrt(0.5))
    C = np.float32(math.cos(math.pi / 8))
    S = np.float32(math.sin(math.pi / 8))
    s = [x[n] + x[n + 8] for n in range(8)]
    d = [x[n] - x[n + 8] for n in range(8)]
    a = [s[n] + s[n + 4] for n in range(4)]
    b = [s[n] - s[n + 4] for n in range(4)]
    out = {}
    a02, a13 = a[0] + a[2], a[1] + a[3]
    out[0] = a02 + a13
    out[8] = a02 - a13
    out[4] = (a[0] - a[2], a[3] - a[1])
    bm, bp = R * (b[1] - b[3]), R * (b[1] + b[3])
    out[2] = (b[0] + bm, -(b[2] + bp))
    out[6] = (b[0] - bm, b[2] - bp)
    e = [None] + [d[n] - d[8 - n] for n in (1, 2, 3)]
    f = [None] + [d[n] + d[8 - n] for n in (1, 2, 3)]
    re2, rf2 = R * e[2], R * f[2]
    p, q = d[0] + re2, d[0] - re2
    u, v = C * e[1] + S * e[3], S * e[1] - C * e[3]
    out[1] = p + u
    out[7] = p - u
    out[3] = q + v
    out[5] = q - v
    w, z = S * f[1] + C * f[3], C * f[1] - S * f[3]
    g, h = rf2 + d[4], rf2 - d[4]
    out[1] = (out[1], -(w + g))
    out[7] = (out[7], g - w)
    out[3] = (out[3], -(z + h))
    out[5] = (out[5], h - z)
    pairs = [(out[0], out[8])] + [out[k] for k in range(1, 8)]
    return pairs


def spectra_kernel(volt, halo, taps, gain, high, low, out, filt, yhi, ylo, spec):
    spec_dev, taps_count = 64, 16
    unroll = 16
    tiles = RADIX

    def pfb_block(n1, half, first):
        cols = lambda m: pl.ds(pl.multiple_of(m * 2048 + n1 * LANES, LANES), LANES)
        rows = slice(half * 8, half * 8 + 8)
        coeff = [
            jnp.broadcast_to(taps[p : p + 1, pl.ds(pl.multiple_of(n1 * LANES, LANES), LANES)], (8, LANES))
            for p in range(taps_count)
        ]
        scale = gain[rows, :]

        def run(m0, frame):
            acc = [None] * unroll
            for s in range(1 - taps_count, unroll):
                value = frame(s)
                for o in range(max(0, s), min(unroll, s + taps_count)):
                    term = coeff[o - s] * value
                    acc[o] = term if acc[o] is None else acc[o] + term
            for o in range(unroll):
                result = (acc[o] * scale).astype(jnp.bfloat16).astype(jnp.float32)
                filt[n1, pl.ds(half * spec_dev + m0 + o, 8, stride=2 * spec_dev), :] = result

        def first_frame(s):
            if s < 0:
                return halo[rows, cols(s + taps_count - 1)].astype(jnp.float32)
            return volt[rows, cols(s)].astype(jnp.float32)

        run(0, first_frame)

        def later(b, carry):
            run(b * unroll, lambda s: volt[rows, cols(b * unroll + s)].astype(jnp.float32))
            return carry

        lax.fori_loop(1, spec_dev // unroll, later, 0)

    def pfb_column(n1, carry):
        for half in range(2):
            pfb_block(n1, half, True)
        return carry

    lax.fori_loop(0, tiles, pfb_column, 0)

    def transform(r, carry):
        base = r * 256

        def coarse(b, inner):
            rows = pl.ds(pl.multiple_of(base + b * 16, 16), 16)
            to = pl.ds(pl.multiple_of(b * 16, 16), 16)
            pairs = real_dft16([filt[n1, rows, :] for n1 in range(RADIX)])
            for g, pair in enumerate(pairs):
                for half, value in enumerate(pair):
                    top = value.astype(jnp.bfloat16)
                    yhi[g, to, half * LANES : half * LANES + LANES] = top
                    ylo[g, to, half * LANES : half * LANES + LANES] = (
                        value - top.astype(jnp.float32)
                    ).astype(jnp.bfloat16)
            return inner

        lax.fori_loop(0, 16, coarse, 0)
        contract = (((1,), (1,)), ((), ()))

        def fine(g, inner):
            dot = functools.partial(
                lax.dot_general, dimension_numbers=contract, preferred_element_type=jnp.float32
            )
            value = dot(high[g], yhi[g]) + (dot(low[g], yhi[g]) + dot(high[g], ylo[g]))
            at = pl.multiple_of(g * 256, 256)
            spec[pl.ds(pl.multiple_of(2 * r * 2048 + at, 256), 256), :] = value[:, :LANES]
            spec[pl.ds(pl.multiple_of((2 * r + 1) * 2048 + at, 256), 256), :] = value[:, LANES:]
            return inner

        lax.fori_loop(0, 8, fine, 0)
        return carry

    lax.fori_loop(0, 4, transform, 0)
    left = lax.broadcasted_iota(jnp.int32, (8, LANES), 1) < 64

    def gather(k2, carry):
        for k1 in range(RADIX):
            h, c = divmod(k1, 8)
            if k1 == 8:
                g, q = 0, 1
            elif k1 > 8:
                g, q = RADIX - k1, 1
            else:
                g, q = k1, 0
            row = g * 256 + q * 128
            re = spec[pl.ds(row + k2, 8, stride=2048), :]
            im = spec[pl.ds(row + 64 + k2, 8, stride=2048), :]
            even = jnp.where(left, re, pltpu.roll(im, 64, 1))
            odd = jnp.where(left, pltpu.roll(re, 64, 1), im)
            out[2 * k2 + h, c] = jnp.concatenate([even, odd], axis=0).astype(jnp.bfloat16)
        return carry

    lax.fori_loop(0, 64, gather, 0)


def correlate_kernel(data, out):
    feeds = data.shape[0]
    parts = []
    turned = []
    for t in range(data.shape[1]):
        part = data[:, t, 0].reshape(feeds * 16, LANES)
        parts.append(part)
        wide = pltpu.roll(part.astype(jnp.float32), 64, 1)
        lane = lax.broadcasted_iota(jnp.int32, wide.shape, 1)
        turned.append(jnp.where(lane < 64, wide, -wide).astype(jnp.bfloat16))
    whole = jnp.concatenate(parts, axis=1)
    other = jnp.concatenate(turned, axis=1)
    contract = (((1,), (1,)), ((), ()))
    out[0, 0] = lax.dot_general(whole, whole, contract, preferred_element_type=jnp.float32) * (1.0 / 256)
    out[0, 1] = lax.dot_general(other, whole, contract, preferred_element_type=jnp.float32) * (1.0 / 256)


def per_device(voltages, pfb_taps, feed_flags):
    inputs_dev, samples_dev = voltages.shape
    taps_count, frame_len = pfb_taps.shape
    high, low = coefficient_tables(frame_len)
    rim = voltages[:, samples_dev - (taps_count - 1) * frame_len :].astype(jnp.bfloat16)
    halo = lax.ppermute(rim, "tm", [(i, i + 1) for i in range(lax.axis_size("tm") - 1)])
    gain = jnp.broadcast_to(feed_flags.astype(jnp.float32)[:, None] * (1.0 / 128), (inputs_dev, LANES))
    vmem = pl.BlockSpec(memory_space=pltpu.VMEM)
    spectra = pl.pallas_call(
        spectra_kernel,
        out_shape=jax.ShapeDtypeStruct((128, 8, 16, LANES), jnp.bfloat16),
        in_specs=[vmem] * 6,
        out_specs=vmem,
        scratch_shapes=[
            pltpu.VMEM((RADIX, 1024, LANES), jnp.float32),
            pltpu.VMEM((8, 256, 256), jnp.bfloat16),
            pltpu.VMEM((8, 256, 256), jnp.bfloat16),
            pltpu.VMEM((8 * 2048, LANES), jnp.float32),
        ],
        compiler_params=pltpu.CompilerParams(vmem_limit_bytes=60 * 2**20),
        name="spectra",
    )(voltages, halo, pfb_taps, gain, jnp.asarray(high), jnp.asarray(low))
    turned = lax.all_to_all(spectra, ("feed", "tm"), split_axis=0, concat_axis=0, tiled=True)
    turned = turned.reshape(32, 4, 8, 16, LANES)
    return pl.pallas_call(
        correlate_kernel,
        out_shape=jax.ShapeDtypeStruct((8, 2, 512, 512), jnp.float32),
        grid=(8,),
        in_specs=[pl.BlockSpec((32, 4, 1, 16, LANES), lambda c: (0, 0, c, 0, 0))],
        out_specs=pl.BlockSpec((1, 2, 512, 512), lambda c: (c, 0, 0, 0)),
        name="correlate",
    )(turned)


def solution(mesh):
    return jax.shard_map(
        per_device,
        mesh=mesh,
        in_specs=(P("feed", "tm"), P(), P("feed")),
        out_specs=P(("feed", "tm"), None, None, None),
        check_vma=False,
    )
```
